32 devices in a mesh: lev: 4 (over y, x), wave: 8 (over z, core).
Axes of the slice: x: 2, y: 2, z: 4, core: 2. Of those that a mesh axis runs over, the one named last changes fastest.
Arguments:
- vorticity: float32 [2, 32, 640, 640], P(None, 'lev', 'wave'), may hold values from -6 to 6
- wind_lam: float32 [32, 640, 1280], P('lev', 'wave'), may hold values from -6 to 6
- wind_mu: float32 [32, 640, 1280], P('lev', 'wave'), may hold values from -6 to 6
- modes: float32 [32, 32], replicated, may hold values from -0.5 to 1.5, as said below
- mode_rates: float32 [32], replicated, may hold values from 0.05 to 2
- wave_order: int32 [640], replicated, may hold values from 0 to 639, each once
- lat_order: int32 [640], replicated, may hold values from 0 to 639, each once
Outputs:
- advanced: float32 [2, 32, 640, 640], P(None, 'lev', 'wave')
- stream: float32 [2, 32, 640, 640], P(None, 'lev', 'wave')
The draws below stay inside these ranges and needn't reach their ends.
Inputs may be any that keep to these rules, and one draw needn't show every extreme that they name: `wave_order`: A permutation: each wavenumber 0 to 639 is held by exactly one slot. `lat_order`: A permutation: each latitude 0 to 639 is held by exactly one slot. `modes`: A dense real matrix.
All inputs are finite; a program needn't handle non-finite values.
Results may differ from the reference program's by a relative error of at most 0.0003.
Values sent between devices are 32-bit elements; how exact they have to be, the bound alone decides.
A program may use at most 320 MiB of HBM per device.

```python
import math
import jax
import jax.numpy as jnp
from jax import lax

M = 640
LAT = 640
GRID_LONGITUDES = 1280
LEV = 32


def draw_modes(key, part):
    noise = jax.random.truncated_normal(key, -2.5, 2.5, (LEV, LEV), jnp.float32)
    return jnp.eye(LEV, dtype=jnp.float32) + 0.6 / math.sqrt(LEV) * noise


def levels(own_key, dims, split, least, top_value):
    gain, own = 1.0, jax.random.fold_in(own_key, 6)
    for position, shards_of in split:
        steps = jnp.exp(jax.random.uniform(jax.random.fold_in(own, position), (shards_of,), jnp.float32, least / len(split), top_value / len(split)))
        gain = gain * jnp.repeat(steps, dims[position] // shards_of).reshape([-1 if axis == position else 1 for axis in range(len(dims))])
    return gain


def bell_draw(rng, shape, spread, most, cuts=(), kind=jnp.bfloat16):
    level = levels(rng, shape, cuts, -0.22, 0.18) if cuts else 1.0
    entries = jax.random.normal(rng, shape, jnp.float32) * spread * level
    return jnp.minimum(jnp.maximum(entries, -most), most).astype(kind)


def setup_inputs(seed: int = 0) -> dict:
    seeds = jax.random.split(jax.random.key(seed), 8)
    vorticity = bell_draw(seeds[0], (2, LEV, M, M), 1.0, 6.0, ((1, 4), (2, 8)), jnp.float32)
    wind_lam = bell_draw(seeds[1], (LEV, LAT, GRID_LONGITUDES), 1.0, 6.0, ((0, 4), (1, 8)), jnp.float32)
    wind_mu = bell_draw(seeds[2], (LEV, LAT, GRID_LONGITUDES), 1.0, 6.0, ((0, 4), (1, 8)), jnp.float32)
    modes = draw_modes(jax.random.fold_in(seeds[7], 71), 0)
    mode_rates = jnp.clip(jnp.exp(jax.random.uniform(seeds[4], (LEV,), jnp.float32, math.log(0.05), math.log(2.0))), 0.05, 2.0)
    wave_order = jax.random.permutation(seeds[5], M).astype(jnp.int32)
    lat_order = jax.random.permutation(seeds[6], LAT).astype(jnp.int32)
    return {"vorticity": vorticity, "wind_lam": wind_lam, "wind_mu": wind_mu, "modes": modes, "mode_rates": mode_rates, "wave_order": wave_order, "lat_order": lat_order}


HIGH_ACCURACY = lax.Precision.HIGHEST
TIME_STEP = 0.4

def latitudes(lat_order):
    angles = math.pi * (lat_order.astype(jnp.float32) + 0.75) / (LAT + 0.5)
    sines = jnp.sin(angles)
    return (jnp.cos(angles), sines, math.pi / (LAT + 0.5) * sines)

def legendre(waves, cosines, sines, degrees):
    wavenum = waves.astype(jnp.float32)[:, None]
    counter = jnp.arange(1, M, dtype=jnp.int32).astype(jnp.float32)
    halves = 0.5 * jnp.log((2.0 * counter + 1.0) / (2.0 * counter))
    start_log = lax.optimization_barrier(jnp.sum(jnp.where(counter[None, :] <= wavenum, halves[None, :], 0.0), axis=1))
    log_start = -0.5 * math.log(2.0) + start_log[:, None] + wavenum * jnp.log(sines)[None, :]

    def advance(carry, step_index):
        previous, current, log_scale = carry
        emitted = current * jnp.exp(log_scale)
        degree = wavenum + step_index.astype(jnp.float32) + 1.0
        factor_ahead = jnp.sqrt((4.0 * degree * degree - 1.0) / (degree * degree - wavenum * wavenum))
        lower_degree = degree - 1.0
        factor_behind = jnp.sqrt((lower_degree * lower_degree - wavenum * wavenum) / (4.0 * lower_degree * lower_degree - 1.0))
        following = factor_ahead * (cosines[None, :] * current - factor_behind * previous)
        magnitude = jnp.abs(current) + jnp.abs(following)
        return ((current / magnitude, following / magnitude, log_scale + jnp.log(magnitude)), emitted)
    initial = (jnp.zeros(log_start.shape, jnp.float32), jnp.ones(log_start.shape, jnp.float32), log_start)
    last_carry, stacked = lax.scan(advance, initial, jnp.arange(degrees, dtype=jnp.int32), unroll=32)
    live_mask = (waves[:, None] + jnp.arange(degrees, dtype=jnp.int32)[None, :] < M).astype(jnp.float32)
    return jnp.transpose(stacked, (1, 0, 2)) * live_mask[:, :, None]

def coupling(waves):
    wavenum = waves.astype(jnp.float32)[:, None]
    degree = wavenum + jnp.arange(M, dtype=jnp.int32).astype(jnp.float32)[None, :]
    live_mask = (degree < M - 0.5).astype(jnp.float32)
    square = wavenum * wavenum
    eps_here = jnp.sqrt((degree * degree - square) / (4.0 * degree * degree - 1.0))
    degree_next = degree + 1.0
    eps_ahead = jnp.sqrt((degree_next * degree_next - square) / (4.0 * degree_next * degree_next - 1.0))
    kappa = degree * (degree + 1.0) / (M * (M + 1.0))
    return (-(degree - 1.0) * eps_here * live_mask, (degree + 2.0) * eps_ahead * live_mask, live_mask, kappa)

def fourier(waves):
    phase = waves[:, None] * jnp.arange(GRID_LONGITUDES, dtype=jnp.int32)[None, :] % GRID_LONGITUDES
    angles = 2.0 * math.pi / GRID_LONGITUDES * phase.astype(jnp.float32)
    return jnp.concatenate([jnp.cos(angles), jnp.sin(angles)], axis=0)

def lowered(spectra):
    return jnp.concatenate([jnp.zeros_like(spectra[..., :1]), spectra[..., :-1]], axis=-1)

def raised(spectra):
    return jnp.concatenate([spectra[..., 1:], jnp.zeros_like(spectra[..., :1])], axis=-1)

def tendency(spectra, waves, cosines, sines, weights, wind_lam, wind_mu, lower, upper, group):
    meridional = lower * lowered(spectra) + upper * raised(spectra)
    both = jnp.stack([spectra, meridional])
    count = M // group

    def inverse_block(index):
        first = index * group
        block_table = legendre(lax.dynamic_slice_in_dim(waves, first, group), cosines, sines, M)
        block_fields = lax.dynamic_slice_in_dim(both, first, group, 3)
        return jnp.einsum('fclsj,sjr->fclsr', block_fields, block_table, precision=HIGH_ACCURACY)
    pieces = lax.map(inverse_block, jnp.arange(count, dtype=jnp.int32))
    at_lat = jnp.moveaxis(pieces, 0, 3).reshape(2, 2, LEV, M, LAT)
    double = jnp.where(waves == 0, 1.0, 2.0).astype(jnp.float32)
    scaled = double * waves.astype(jnp.float32)
    zonal = jnp.concatenate([-(scaled[:, None] * at_lat[0, 1]), -(scaled[:, None] * at_lat[0, 0])], axis=1)
    merid = jnp.concatenate([double[:, None] * at_lat[1, 0], -(double[:, None] * at_lat[1, 1])], axis=1)
    trigonometric_table = fourier(waves)
    grid = jnp.einsum('flsr,sk->flrk', jnp.stack([zonal, merid]), trigonometric_table, precision=HIGH_ACCURACY)
    source_term = -(wind_lam * grid[0] + wind_mu * grid[1])
    spectral_latitude_fields = jnp.einsum('nqy,zy->nzq', source_term, trigonometric_table, precision=HIGH_ACCURACY) / GRID_LONGITUDES
    returned = jnp.stack([spectral_latitude_fields[:, :M], -spectral_latitude_fields[:, M:]]) * weights

    def forward_block(index):
        first = index * group
        block_table = legendre(lax.dynamic_slice_in_dim(waves, first, group), cosines, sines, M)
        block_fields = lax.dynamic_slice_in_dim(returned, first, group, 2)
        return jnp.einsum('clsr,sjr->clsj', block_fields, block_table, precision=HIGH_ACCURACY)
    pieces = lax.map(forward_block, jnp.arange(count, dtype=jnp.int32))
    return jnp.moveaxis(pieces, 0, 2).reshape(2, LEV, M, M)

def reference(vorticity, wind_lam, wind_mu, modes, mode_rates, wave_order, lat_order):
    cosines, sines, weights = latitudes(lat_order)
    lower, upper, live_mask, kappa = coupling(wave_order)
    group = math.gcd(M, 64)
    start = vorticity * live_mask
    first_rate = tendency(start, wave_order, cosines, sines, weights, wind_lam, wind_mu, lower, upper, group)
    middle = start + TIME_STEP / M * first_rate
    second_rate = tendency(middle, wave_order, cosines, sines, weights, wind_lam, wind_mu, lower, upper, group)
    advanced = start + 0.5 * TIME_STEP / M * (first_rate + second_rate)
    projected = jnp.einsum('lk,clsj->cksj', modes, advanced, precision=HIGH_ACCURACY)
    projected = projected / (kappa[None, None] + mode_rates[None, :, None, None])
    stream = jnp.einsum('lk,cksj->clsj', modes, projected, precision=HIGH_ACCURACY) * live_mask
    return (advanced, stream)
```

```python
import functools
import math

import jax
import jax.numpy as jnp
from jax import lax
from jax.experimental import pallas as pl
from jax.experimental.pallas import tpu as pltpu
from jax.sharding import PartitionSpec as P
import numpy as np

M = 640
LAT = 640
GRID_LONGITUDES = 1280


HIGH_ACCURACY = lax.Precision.HIGH
TIME_STEP = 0.4


def latitudes(lat_order):
    angles = math.pi * (lat_order.astype(jnp.float32) + 0.75) / (LAT + 0.5)
    sines = jnp.sin(angles)
    return (jnp.cos(angles), sines, math.pi / (LAT + 0.5) * sines)


GROUP = 8
PARTS = 2
LANES = 128
VMEM = 60 * 1024 * 1024


def table_kernel(ahead_ref, behind_ref, start_ref, cos_ref, out_ref):
    lats = out_ref.shape[2]
    spans = [(k, min(LANES, lats - k)) for k in range(0, lats, LANES)]
    mus = [jnp.broadcast_to(cos_ref[0:1, k : k + n], (GROUP, n)) for k, n in spans]

    def block(index, carry):
        first = pl.multiple_of(index * 8, 8)
        ahead = [ahead_ref[first + t] for t in range(8)]
        behind = [behind_ref[first + t] for t in range(8)]
        following_carry = []
        for (k, n), mu, (previous, current, log_scale) in zip(spans, mus, carry):
            scale = jnp.exp(log_scale)
            rows = []
            for t in range(8):
                rows.append(current * scale)
                following = ahead[t][:, :n] * (mu * current - behind[t][:, :n] * previous)
                previous, current = current, following
            magnitude = jnp.abs(previous) + jnp.abs(current)
            following_carry.append(
                (previous / magnitude, current / magnitude, log_scale + jnp.log(magnitude))
            )
            out_ref[:, pl.ds(first, 8), k : k + n] = jnp.swapaxes(jnp.stack(rows), 0, 1)
        return tuple(following_carry)

    initial = tuple(
        (
            jnp.zeros((GROUP, n), jnp.float32),
            jnp.ones((GROUP, n), jnp.float32),
            start_ref[:, k : k + n],
        )
        for k, n in spans
    )
    lax.fori_loop(0, out_ref.shape[1] // 8, block, initial)


def legendre(waves, cosines, sines, degrees):
    wavenum = waves.astype(jnp.float32)[:, None]
    counter = jnp.arange(1, M, dtype=jnp.int32).astype(jnp.float32)
    halves = 0.5 * jnp.log((2.0 * counter + 1.0) / (2.0 * counter))
    start_log = jnp.sum(jnp.where(counter[None, :] <= wavenum, halves[None, :], 0.0), axis=1)
    log_start = -0.5 * math.log(2.0) + start_log[:, None] + wavenum * jnp.log(sines)[None, :]
    degree = wavenum.T + jnp.arange(degrees, dtype=jnp.int32).astype(jnp.float32)[:, None] + 1.0
    square = wavenum.T * wavenum.T
    ahead = jnp.sqrt((4.0 * degree * degree - 1.0) / (degree * degree - square))
    lower = degree - 1.0
    behind = jnp.sqrt((lower * lower - square) / (4.0 * lower * lower - 1.0))
    slots, lats = waves.shape[0], cosines.shape[0]
    wide = (degrees, slots, LANES)
    coefficient = pl.BlockSpec((degrees, GROUP, LANES), lambda g: (0, g, 0))
    return pl.pallas_call(
        table_kernel,
        grid=(slots // GROUP,),
        in_specs=[
            coefficient,
            coefficient,
            pl.BlockSpec((GROUP, lats), lambda g: (g, 0)),
            pl.BlockSpec((1, lats), lambda g: (0, 0)),
        ],
        out_specs=pl.BlockSpec((GROUP, degrees, lats), lambda g: (g, 0, 0)),
        out_shape=jax.ShapeDtypeStruct((slots, degrees, lats), jnp.float32),
        compiler_params=pltpu.CompilerParams(vmem_limit_bytes=VMEM),
        name="table",
    )(
        jnp.broadcast_to(ahead[:, :, None], wide),
        jnp.broadcast_to(behind[:, :, None], wide),
        log_start,
        cosines[None, :],
    )


def halves_of(value):
    high = value.astype(jnp.bfloat16)
    return high, (value - high.astype(jnp.float32)).astype(jnp.bfloat16)


def three_products(fields, table, contract):
    rows = fields.shape[0]
    field_high, field_low = halves_of(fields)
    table_high, table_low = halves_of(table)
    dims = (((1,), (contract,)), ((), ()))
    both = lax.dot_general(
        jnp.concatenate([field_high, field_low], axis=0),
        table_high,
        dims,
        preferred_element_type=jnp.float32,
    )
    small = lax.dot_general(field_high, table_low, dims, preferred_element_type=jnp.float32)
    return both[:rows] + (both[rows:] + small)


def transform_kernel(waves_ref, fields_ref, table_ref, after_ref, out_ref, turned, result, *, forward):
    degrees = table_ref.shape[1]
    turned[...] = jnp.swapaxes(fields_ref[...], 0, 1)
    group = pl.program_id(0)

    def one_slot(i, carry):
        alive = degrees - waves_ref[group * GROUP + i]
        for first in range(0, degrees, 256):
            last = min(first + 256, degrees)

            @pl.when(alive > first)
            def _():
                table = table_ref[i, first:last, :]
                if forward:
                    result[i, :, first:last] = three_products(turned[i], table, 1)
                elif first == 0:
                    result[i] = three_products(turned[i, :, first:last], table, 0)
                else:
                    result[i] += three_products(turned[i, :, first:last], table, 0)

            if forward:

                @pl.when(alive <= first)
                def _():
                    result[i, :, first:last] = jnp.zeros(
                        (result.shape[1], last - first), jnp.float32
                    )

        return carry

    lax.fori_loop(0, GROUP, one_slot, 0)
    out_ref[...] = jnp.swapaxes(result[...], 0, 1)


def transform(waves, fields, table, after, forward):
    rows, slots, width = fields.shape
    degrees, lats = table.shape[1:]
    out_width = degrees if forward else lats
    return pl.pallas_call(
        functools.partial(transform_kernel, forward=forward),
        grid_spec=pltpu.PrefetchScalarGridSpec(
            num_scalar_prefetch=1,
            grid=(slots // GROUP,),
            in_specs=[
                pl.BlockSpec((rows, GROUP, width), lambda g, w: (0, g, 0)),
                pl.BlockSpec((GROUP, degrees, lats), lambda g, w: (g, 0, 0)),
                pl.BlockSpec(memory_space=pl.ANY),
            ],
            out_specs=pl.BlockSpec((rows, GROUP, out_width), lambda g, w: (0, g, 0)),
            scratch_shapes=[
                pltpu.VMEM((GROUP, rows, width), jnp.float32),
                pltpu.VMEM((GROUP, rows, out_width), jnp.float32),
            ],
        ),
        out_shape=jax.ShapeDtypeStruct((rows, slots, out_width), jnp.float32),
        compiler_params=pltpu.CompilerParams(vmem_limit_bytes=VMEM),
        name="analysis" if forward else "synthesis",
    )(waves, fields, table, after)


def padded(array, axis, size):
    widths = [(0, 0)] * array.ndim
    widths[axis] = (0, size - array.shape[axis])
    return jnp.pad(array, widths) if size > array.shape[axis] else array


def coupling(waves):
    wavenum = waves.astype(jnp.float32)[:, None]
    degree = wavenum + jnp.arange(M, dtype=jnp.int32).astype(jnp.float32)[None, :]
    live_mask = (degree < M - 0.5).astype(jnp.float32)
    square = wavenum * wavenum
    eps_here = jnp.sqrt((degree * degree - square) / (4.0 * degree * degree - 1.0))
    degree_next = degree + 1.0
    eps_ahead = jnp.sqrt(
        (degree_next * degree_next - square) / (4.0 * degree_next * degree_next - 1.0)
    )
    kappa = degree * (degree + 1.0) / (M * (M + 1.0))
    return (
        -(degree - 1.0) * eps_here * live_mask,
        (degree + 2.0) * eps_ahead * live_mask,
        live_mask,
        kappa,
    )


def fourier(waves):
    phase = waves[:, None] * jnp.arange(GRID_LONGITUDES, dtype=jnp.int32)[None, :] % GRID_LONGITUDES
    angles = 2.0 * math.pi / GRID_LONGITUDES * phase.astype(jnp.float32)
    return jnp.concatenate([jnp.cos(angles), jnp.sin(angles)], axis=0)


def lowered(spectra):
    return jnp.concatenate([jnp.zeros_like(spectra[..., :1]), spectra[..., :-1]], axis=-1)


def raised(spectra):
    return jnp.concatenate([spectra[..., 1:], jnp.zeros_like(spectra[..., :1])], axis=-1)


def on_device(vorticity, wind_lam, wind_mu, modes, mode_rates, wave_order, lat_order):
    slots = vorticity.shape[2]
    wave_pos = lax.axis_index("wave")
    lev_pos = lax.axis_index("lev")
    waves = lax.dynamic_slice_in_dim(wave_order, wave_pos * slots, slots)
    cosines, sines, weights = latitudes(lat_order)
    full = -(-slots // GROUP) * GROUP
    full_waves = padded(waves, 0, full)
    legendre_table = legendre(full_waves, cosines, sines, M)
    lower, upper, live_mask, kappa = coupling(waves)
    trigonometric_table = fourier(wave_order)
    double = jnp.where(wave_order == 0, 1.0, 2.0).astype(jnp.float32)
    scaled = double * wave_order.astype(jnp.float32)

    def synthesis(spectra, after):
        meridional = lower * lowered(spectra) + upper * raised(spectra)
        both = jnp.stack([spectra, meridional])
        rows = both.shape[0] * both.shape[1] * both.shape[2]
        flat = padded(both.reshape(rows, slots, M), 1, full)
        at_lat = transform(full_waves, flat, legendre_table, after, False)[:, :slots]
        return at_lat.reshape(both.shape[:4] + (LAT,))

    def to_latitudes(at_lat):
        return lax.all_to_all(at_lat, "wave", split_axis=4, concat_axis=3, tiled=True)

    def products(at_lat, part_lam, part_mu):
        zonal = jnp.concatenate(
            [-(scaled[:, None] * at_lat[0, 1]), -(scaled[:, None] * at_lat[0, 0])], axis=1
        )
        merid = jnp.concatenate(
            [double[:, None] * at_lat[1, 0], -(double[:, None] * at_lat[1, 1])], axis=1
        )
        grid = jnp.einsum(
            "flsr,sk->flrk", jnp.stack([zonal, merid]), trigonometric_table, precision=HIGH_ACCURACY
        )
        source_term = -(part_lam * grid[0] + part_mu * grid[1])
        spectral_latitude_fields = (
            jnp.einsum("nqy,zy->nzq", source_term, trigonometric_table, precision=HIGH_ACCURACY)
            / GRID_LONGITUDES
        )
        return jnp.stack([spectral_latitude_fields[:, :M], -spectral_latitude_fields[:, M:]])

    def to_waves(returned):
        return lax.all_to_all(returned, "wave", split_axis=2, concat_axis=3, tiled=True)

    def analysis(returned, after):
        returned = returned * weights
        flat = padded(returned.reshape(-1, slots, LAT), 1, full)
        result = transform(full_waves, flat, legendre_table, after, True)[:, :slots]
        return result.reshape(returned.shape[:3] + (M,)) * live_mask

    def token(array):
        corner = array[(0,) * (array.ndim - 2)]
        return lax.slice(corner, (0, 0), (min(8, corner.shape[0]), min(LANES, corner.shape[1])))

    def ordered(array, earlier):
        return array + 0.0 * token(earlier)[0, 0]

    levels = vorticity.shape[1]
    step = levels // PARTS if levels % PARTS == 0 else levels
    parts = [slice(first, first + step) for first in range(0, levels, step)]
    lev_count = modes.shape[0] // levels
    grouped = modes.reshape(lev_count, levels, modes.shape[1])
    rows_of = [grouped[:, part].reshape(lev_count * step, -1) for part in parts]
    winds = [(wind_lam[part], wind_mu[part]) for part in parts]
    starts = [vorticity[:, part] * live_mask for part in parts]
    count = len(parts)
    last = cosines[None, :]

    at_lats = []
    for start in starts:
        at_lats.append(synthesis(start, last))
        last = token(at_lats[-1])
    landed = [token(cosines[None, None, :])]

    def in_turn(exchange, array):
        moved = exchange(ordered(array, landed[0]))
        landed[0] = token(moved)
        return moved

    at_lats = [in_turn(to_latitudes, at_lat) for at_lat in at_lats]
    rates = []
    for stage in range(2):
        returned = []
        for at_lat, wind in zip(at_lats, winds):
            returned.append(products(ordered(at_lat, last), *wind))
            last = token(returned[-1])
        returned = [in_turn(to_waves, piece) for piece in returned]
        at_lats = []
        for index in range(count):
            rate = analysis(returned[index], last)
            last = token(rate)
            rates.append(rate)
            if stage == 0:
                middle = starts[index] + TIME_STEP / M * rate
                at_lats.append(synthesis(middle, last))
                last = token(at_lats[-1])
        at_lats = [in_turn(to_latitudes, at_lat) for at_lat in at_lats]
    advanced_parts = [
        starts[index] + 0.5 * TIME_STEP / M * (rates[index] + rates[count + index])
        for index in range(count)
    ]
    def to_blocks(array):
        return lax.all_to_all(array, "lev", split_axis=3, concat_axis=1, tiled=True)

    projected = 0.0
    for advanced, rows in zip(advanced_parts, rows_of):
        gathered = in_turn(to_blocks, advanced)
        projected = projected + jnp.einsum(
            "lk,clsj->cksj", rows, gathered, precision=HIGH_ACCURACY
        )
    block_width = projected.shape[3]
    diffusion_block = lax.dynamic_slice_in_dim(kappa, lev_pos * block_width, block_width, 1)
    projected = projected / (diffusion_block[None, None] + mode_rates[None, :, None, None])
    streams = []
    for rows in rows_of:
        restored = jnp.einsum("lk,cksj->clsj", rows, projected, precision=HIGH_ACCURACY)
        streams.append(lax.all_to_all(restored, "lev", split_axis=1, concat_axis=3, tiled=True))
    advanced = jnp.concatenate(advanced_parts, axis=1)
    stream = jnp.concatenate(streams, axis=1) * live_mask
    return (advanced, stream)


def order_list(size):
    blocks = size // (2 * GROUP)
    first = np.arange(blocks // 2)[:, None, None]
    block = np.concatenate([first, blocks - 1 - first], axis=1)
    return (block * GROUP + np.arange(GROUP)[None, None, :]).astype(np.int32)


def packed_width(size):
    width = size + 2 * GROUP
    return width, -(-width // LANES) * LANES


def packed_coupling(parity, size):
    width, lanes = packed_width(size)
    orders = 2 * jnp.asarray(order_list(size)) + parity
    lane = lax.broadcasted_iota(jnp.int32, (orders.shape[0], GROUP, lanes), 2)
    split = size - 2 * GROUP * lax.broadcasted_iota(jnp.int32, lane.shape, 0)
    wave = jnp.where(lane < split, orders[:, 0, :, None], orders[:, 1, :, None])
    degree = wave + jnp.where(lane < split, lane, lane - split)
    live = (degree < size) & (lane < width)
    ahead_live = (degree + 1 < size) & (lane < width)
    wave, degree = wave.astype(jnp.float32), degree.astype(jnp.float32)
    square = wave * wave
    following = degree + 1.0
    here = jnp.sqrt((degree * degree - square) / (4.0 * degree * degree - 1.0))
    beyond = jnp.sqrt((following * following - square) / (4.0 * following * following - 1.0))
    lower = jnp.where(live, -(degree - 1.0) * here, 0.0)
    upper = jnp.where(ahead_live, (degree + 2.0) * beyond, 0.0)
    ahead = jnp.sqrt(
        (4.0 * following * following - 1.0) / (following * following - square)
    )
    return lower, upper, live.astype(jnp.float32), ahead, here


def half_table_kernel(coefficient_ref, start_ref, cos_ref, high_ref, low_ref, *, size):
    lats = cos_ref.shape[1]
    pair = pl.program_id(0)
    spans = [(k, min(LANES, lats - k)) for k in range(0, lats, LANES)]
    mus = [jnp.broadcast_to(cos_ref[0:1, k : k + n], (GROUP, n)) for k, n in spans]
    blocks = coefficient_ref.shape[1]
    restart = size // 16 - pair

    def fresh(which, k, n):
        return (
            jnp.zeros((GROUP, n), jnp.float32),
            jnp.ones((GROUP, n), jnp.float32),
            start_ref[0, which, :, k : k + n],
        )

    def block(index, carry):
        first = pl.multiple_of(index * 16, 16)
        again = index == restart
        coefficients = coefficient_ref[0, index]
        ahead = [jnp.broadcast_to(coefficients[:, t : t + 1], (GROUP, LANES)) for t in range(16)]
        behind = [
            jnp.broadcast_to(coefficients[:, 16 + t : 17 + t], (GROUP, LANES)) for t in range(16)
        ]
        following_carry = []
        for (k, n), mu, old in zip(spans, mus, carry):
            previous, current, log_scale = [
                jnp.where(again, new, kept) for new, kept in zip(fresh(1, k, n), old)
            ]
            rows = []
            for t in range(16):
                if t % 8 == 0:
                    scale = jnp.exp(log_scale)
                rows.append(current * scale)
                following = ahead[t][:, :n] * (mu * current - behind[t][:, :n] * previous)
                previous, current = current, following
                if t % 8 == 7:
                    magnitude = jnp.abs(previous) + jnp.abs(current)
                    inverse = 1.0 / magnitude
                    previous, current = previous * inverse, current * inverse
                    log_scale = log_scale + jnp.log(magnitude)
            following_carry.append((previous, current, log_scale))
            values = jnp.concatenate(
                [
                    jnp.swapaxes(jnp.stack(rows[:8]), 0, 1),
                    jnp.swapaxes(jnp.stack(rows[8:]), 0, 1),
                ],
                axis=1,
            )
            high = values.astype(jnp.bfloat16)
            high_ref[0, :, pl.ds(first, 16), k : k + n] = high
            low_ref[0, :, pl.ds(first, 16), k : k + n] = (
                values - high.astype(jnp.float32)
            ).astype(jnp.bfloat16)
        return tuple(following_carry)

    lax.fori_loop(0, blocks, block, tuple(fresh(0, k, n) for k, n in spans))


def half_table(parity, cosines, sines, ahead, behind, size):
    width, _ = packed_width(size)
    orders = 2 * jnp.asarray(order_list(size)) + parity
    pairs, lats = orders.shape[0], cosines.shape[0]
    wavenum = orders.reshape(-1).astype(jnp.float32)[:, None]
    counter = jnp.arange(1, size, dtype=jnp.int32).astype(jnp.float32)
    halves = 0.5 * jnp.log((2.0 * counter + 1.0) / (2.0 * counter))
    start_log = jnp.sum(jnp.where(counter[None, :] <= wavenum, halves[None, :], 0.0), axis=1)
    log_start = -0.5 * math.log(2.0) + start_log[:, None] + wavenum * jnp.log(sines)[None, :]
    log_start = log_start.reshape(pairs, 2, GROUP, lats)
    blocks = width // 16

    def by_block(array):
        return jnp.swapaxes(array[:, :, :width].reshape(pairs, GROUP, blocks, 16), 1, 2)

    coefficients = jnp.concatenate([by_block(ahead), by_block(behind)], axis=3)
    table = jax.ShapeDtypeStruct((pairs, GROUP, width, lats), jnp.bfloat16)
    table_spec = pl.BlockSpec((1, GROUP, width, lats), lambda g: (g, 0, 0, 0))
    return pl.pallas_call(
        functools.partial(half_table_kernel, size=size),
        grid=(pairs,),
        in_specs=[
            pl.BlockSpec((1, blocks, GROUP, 32), lambda g: (g, 0, 0, 0)),
            pl.BlockSpec((1, 2, GROUP, lats), lambda g: (g, 0, 0, 0)),
            pl.BlockSpec((1, lats), lambda g: (0, 0)),
        ],
        out_specs=[table_spec, table_spec],
        out_shape=[table, table],
        compiler_params=pltpu.CompilerParams(vmem_limit_bytes=VMEM),
        cost_estimate=pl.CostEstimate(
            flops=pairs * GROUP * width * lats * 10,
            bytes_accessed=pairs * GROUP * width * lats * 4,
            transcendentals=0,
        ),
        name="half_table",
    )(coefficients, log_start, cosines[None, :])


def split_halves(value):
    high = value.astype(jnp.bfloat16)
    return high, (value - high.astype(jnp.float32)).astype(jnp.bfloat16)


def visit_kernel(*refs, size, stage):
    refs = list(refs)
    high_ref, low_ref = refs.pop(0), refs.pop(0)
    pair = pl.program_id(0)
    width, lanes = packed_width(size)
    split = size - 2 * GROUP * pair
    lats = high_ref.shape[3]
    position = lax.broadcasted_iota(jnp.int32, (1, lanes), 1)
    in_first, even = position < split, position % 2 == 0
    picks = [in_first & even, in_first & ~even, ~in_first & even, ~in_first & ~even]
    step = TIME_STEP / size

    def multiply(fields, table_slot, chunks, contract):
        rows = fields.shape[0]
        field_high, field_low = split_halves(fields)
        both_fields = jnp.concatenate([field_high, field_low], axis=0)
        both = small = None
        dims = (((1,), (contract,)), ((), ()))
        for c0, c1 in chunks:
            table_high = high_ref[0, table_slot, c0:c1, :]
            table_low = low_ref[0, table_slot, c0:c1, :]
            if contract == 0:
                left, left_high = both_fields[:, c0:c1], field_high[:, c0:c1]
            else:
                left, left_high = both_fields, field_high
            part = lax.dot_general(left, table_high, dims, preferred_element_type=jnp.float32)
            part_small = lax.dot_general(
                left_high, table_low, dims, preferred_element_type=jnp.float32
            )
            if both is None:
                both, small = [part], [part_small]
            elif contract == 0:
                both, small = [both[0] + part], [small[0] + part_small]
            else:
                both, small = both + [part], small + [part_small]
        both = jnp.concatenate(both, axis=1) if len(both) > 1 else both[0]
        small = jnp.concatenate(small, axis=1) if len(small) > 1 else small[0]
        return both[:rows] + (both[rows:] + small)

    chunks = [(c0, min(c0 + 256, width)) for c0 in range(0, width, 256)]

    if stage != "last":
        lower_ref, upper_ref = refs.pop(0), refs.pop(0)
    live_ref = refs.pop(0)
    if stage == "first":
        own_q_ref, other_q_ref, start_ref, own_ref, other_ref, fields, firsts, seconds = refs
        padding = jnp.zeros((4, lanes - size), jnp.float32)
        fields[0] = jnp.swapaxes(own_q_ref[:, 0, 0], 0, 1)
        fields[1] = jnp.swapaxes(other_q_ref[:, 0, 0], 0, 1)
        fields[2] = jnp.swapaxes(own_q_ref[:, 0, 1], 0, 1)
        fields[3] = jnp.swapaxes(other_q_ref[:, 0, 1], 0, 1)
    elif stage == "middle":
        own_b_ref, other_b_ref, start_ref, rate_ref, own_ref, other_ref, fields, firsts, seconds = refs
    else:
        own_b_ref, other_b_ref, start_ref, rate_ref, own_ref, other_ref, fields, firsts, seconds = refs
    if stage != "first":
        fields[0] = jnp.swapaxes(own_b_ref[:, 0, 0], 0, 1)
        fields[1] = jnp.swapaxes(other_b_ref[:, 0, 0], 0, 1)
        fields[2] = jnp.swapaxes(own_b_ref[:, 0, 1], 0, 1)
        fields[3] = jnp.swapaxes(other_b_ref[:, 0, 1], 0, 1)

    def one_slot(slot, carry):
        live = live_ref[0, pl.ds(slot, 1), :]
        block_a = jnp.concatenate([fields[0, slot], fields[1, slot]], axis=0)
        block_b = jnp.concatenate([fields[2, slot], fields[3, slot]], axis=0)
        if stage == "first":
            block_a = jnp.concatenate([block_a, padding], axis=1)
            block_b = pltpu.roll(jnp.concatenate([block_b, padding], axis=1), split, 1)
            spectra = jnp.where(in_first, block_a, block_b) * live
            start_ref[0, slot] = spectra
        else:
            sides = []
            for block in (block_a, block_b):
                north, south = block[:, :lats], block[:, lats:]
                sides += [north + south, north - south]
            sums = multiply(jnp.concatenate(sides, axis=0), slot, chunks, 1)
            sums = jnp.concatenate(
                [sums, jnp.zeros((sums.shape[0], lanes - width), jnp.float32)], axis=1
            )
            rate = jnp.zeros((4, lanes), jnp.float32)
            for index, pick in enumerate(picks):
                rate = jnp.where(pick, sums[4 * index : 4 * index + 4], rate)
            rate = rate * live
            if stage == "middle":
                rate_ref[0, slot] = rate
                spectra = start_ref[0, slot] + step * rate
            else:
                spectra = start_ref[0, slot] + 0.5 * step * (rate_ref[0, slot] + rate)
        if stage == "last":
            firsts[slot, :4] = jnp.where(in_first, spectra, 0.0)[:, :size]
            turned = pltpu.roll(spectra, lanes - split, 1)
            seconds[slot, :4] = jnp.where(position < width - split, turned, 0.0)[:, :size]
        else:
            meridional = lower_ref[0, pl.ds(slot, 1), :] * pltpu.roll(
                spectra, 1, 1
            ) + upper_ref[0, pl.ds(slot, 1), :] * pltpu.roll(spectra, lanes - 1, 1)
            both = jnp.concatenate([spectra, meridional], axis=0)
            masked = jnp.concatenate([jnp.where(pick, both, 0.0) for pick in picks], axis=0)
            sums = multiply(masked, slot, chunks, 0)
            firsts[slot] = jnp.concatenate([sums[0:8] + sums[8:16], sums[0:8] - sums[8:16]], axis=1)
            seconds[slot] = jnp.concatenate(
                [sums[16:24] + sums[24:32], sums[16:24] - sums[24:32]], axis=1
            )
        return carry

    lax.fori_loop(0, GROUP, one_slot, 0)
    for which, result in ((0, firsts), (1, seconds)):
        turned = jnp.swapaxes(result[...], 0, 1)
        if stage == "last":
            own_ref[:, 0, which] = turned[0:2]
            other_ref[:, 0, which] = turned[2:4]
        else:
            own_ref[0:2, 0, which] = turned[0:2]
            own_ref[2:4, 0, which] = turned[4:6]
            other_ref[0:2, 0, which] = turned[2:4]
            other_ref[2:4, 0, which] = turned[6:8]


def visit(stage, table, tables, arrays, size):
    width, lanes = packed_width(size)
    pairs, lats = table[0].shape[0], table[0].shape[3]
    table_spec = pl.BlockSpec((1, GROUP, width, lats), lambda g: (g, 0, 0, 0))
    row_spec = pl.BlockSpec((1, GROUP, lanes), lambda g: (g, 0, 0))
    packed_spec = pl.BlockSpec((1, GROUP, 4, lanes), lambda g: (g, 0, 0, 0))
    packed = jax.ShapeDtypeStruct((pairs, GROUP, 4, lanes), jnp.float32)

    def slots_spec(rows, columns):
        return pl.BlockSpec((rows, 1, 2, GROUP, columns), lambda g: (0, g, 0, 0, 0))

    def slots_shape(rows, columns):
        return jax.ShapeDtypeStruct((rows, pairs, 2, GROUP, columns), jnp.float32)

    at_lat = [slots_spec(4, 2 * lats)] * 2
    at_lat_shape = [slots_shape(4, 2 * lats)] * 2
    if stage == "first":
        in_columns, out_columns, out_rows = size, 2 * lats, 8
        specs = [row_spec] * 3 + [slots_spec(2, size)] * 2
        out_specs, out_shape = [packed_spec] + at_lat, [packed] + at_lat_shape
    elif stage == "middle":
        in_columns, out_columns, out_rows = 2 * lats, 2 * lats, 8
        specs = [row_spec] * 3 + [slots_spec(2, 2 * lats)] * 2 + [packed_spec]
        out_specs, out_shape = [packed_spec] + at_lat, [packed] + at_lat_shape
    else:
        in_columns, out_columns, out_rows = 2 * lats, size, 4
        specs = [row_spec] + [slots_spec(2, 2 * lats)] * 2 + [packed_spec] * 2
        out_specs, out_shape = [slots_spec(2, size)] * 2, [slots_shape(2, size)] * 2
    return pl.pallas_call(
        functools.partial(visit_kernel, size=size, stage=stage),
        grid=(pairs,),
        in_specs=[table_spec] * 2 + specs,
        out_specs=out_specs,
        out_shape=out_shape,
        scratch_shapes=[
            pltpu.VMEM((4, GROUP, 2, in_columns), jnp.float32),
            pltpu.VMEM((GROUP, out_rows, out_columns), jnp.float32),
            pltpu.VMEM((GROUP, out_rows, out_columns), jnp.float32),
        ],
        compiler_params=pltpu.CompilerParams(vmem_limit_bytes=VMEM),
        cost_estimate=pl.CostEstimate(
            flops=pairs * GROUP * width * lats * 200,
            bytes_accessed=pairs * GROUP * width * lats * 4,
            transcendentals=0,
        ),
        name="visit_" + stage,
    )(*table, *tables, *arrays)


def by_level(vorticity, wind_lam, wind_mu, modes, mode_rates, wave_order, lat_order):
    comps, levels, slots, size = vorticity.shape
    lat_slots, longitudes = wind_lam.shape[1:]
    lats = lat_order.shape[0]
    half_lats, half_lons = lats // 2, longitudes // 2
    devices = levels
    wave_pos = lax.axis_index("wave")
    lev_pos = lax.axis_index("lev")
    parity = wave_pos % 2
    swap = [(d, d ^ 1) for d in range(devices)]

    def exchange(array):
        return lax.ppermute(array, "wave", swap)

    def to_levels(array):
        return lax.all_to_all(array, "wave", split_axis=0, concat_axis=0, tiled=True)

    every = jnp.arange(size, dtype=jnp.int32)
    slot_of = jnp.zeros((size,), jnp.int32).at[wave_order].set(every)
    lat_slot_of = jnp.zeros((lats,), jnp.int32).at[lat_order].set(
        jnp.arange(lats, dtype=jnp.int32)
    )
    order = order_list(size)
    pairs = order.shape[0]
    flat_order = jnp.asarray(order.reshape(-1))

    spread = to_levels(jnp.swapaxes(vorticity, 0, 1)).reshape(devices * comps * slots, size)

    def rows_of(which):
        slot = jnp.take(slot_of, 2 * flat_order + which)
        row = (slot // slots) * (comps * slots) + slot % slots
        rows = jnp.take(spread, jnp.concatenate([row, row + slots]), axis=0)
        return rows.reshape(comps, pairs, 2, GROUP, size)

    north = jnp.arange(half_lats, dtype=jnp.int32)
    cosines, sines, weights = latitudes(north)
    lower, upper, live, ahead, behind = packed_coupling(parity, size)
    table = half_table(parity, cosines, sines, ahead, behind, size)

    lat_rows = jnp.take(lat_slot_of, jnp.concatenate([north, lats - 1 - north]))

    def wind_of(wind):
        rows = to_levels(wind).reshape(lats, longitudes)
        return jnp.take(rows, lat_rows, axis=0)

    sign = 1.0 - 2.0 * parity.astype(jnp.float32)
    row_scale = jnp.concatenate([weights, weights])[:, None] / longitudes

    def trigonometric(which):
        waves = 2 * flat_order + which
        phase = waves[:, None] * jnp.arange(half_lons, dtype=jnp.int32)[None, :] % longitudes
        angles = 2.0 * math.pi / longitudes * phase.astype(jnp.float32)
        cos, sin = jnp.cos(angles), jnp.sin(angles)
        double = jnp.where(waves == 0, 1.0, 2.0).astype(jnp.float32)[:, None]
        scaled = double * waves.astype(jnp.float32)[:, None]
        zonal = jnp.concatenate([-scaled * sin, -scaled * cos], axis=0)
        merid = jnp.concatenate([double * cos, -double * sin], axis=0)
        back = jnp.concatenate([cos, -sin], axis=0)
        return zonal, merid, back

    trig_own, trig_other = trigonometric(parity), trigonometric(1 - parity)

    def tendency_rows(own, other, wind_l, wind_m):
        received = exchange(other)

        def grid(field, table_own, table_other):
            mine = own[2 * field : 2 * field + 2].reshape(size, lats)
            theirs = received[2 * field : 2 * field + 2].reshape(size, lats)
            here = jnp.einsum("sr,sk->rk", mine, table_own, precision=HIGH_ACCURACY)
            there = jnp.einsum("sr,sk->rk", theirs, table_other, precision=HIGH_ACCURACY)
            return here + there, sign * (here - there)

        lam_near, lam_far = grid(0, trig_own[0], trig_other[0])
        mu_near, mu_far = grid(1, trig_own[1], trig_other[1])
        near = -(wind_l[:, :half_lons] * lam_near + wind_m[:, :half_lons] * mu_near) * row_scale
        far = -(wind_l[:, half_lons:] * lam_far + wind_m[:, half_lons:] * mu_far) * row_scale
        far = sign * far

        def back(folded, table_back):
            rows = jnp.einsum("zk,rk->zr", table_back, folded, precision=HIGH_ACCURACY)
            return rows.reshape(comps, pairs, 2, GROUP, lats)

        other_rows = exchange(back(near - far, trig_other[2]))
        own_rows = back(near + far, trig_own[2])
        return own_rows, other_rows

    own_q, other_q = rows_of(parity), exchange(rows_of(1 - parity))
    start, own_a, other_a = visit("first", table, [lower, upper, live], [own_q, other_q], size)
    wind_l, wind_m = wind_of(wind_lam), wind_of(wind_mu)
    own_b, other_b = tendency_rows(own_a, other_a, wind_l, wind_m)
    first_rate, own_a, other_a = visit(
        "middle", table, [lower, upper, live], [own_b, other_b, start], size
    )
    own_b, other_b = tendency_rows(own_a, other_a, wind_l, wind_m)
    own_q, other_q = visit("last", table, [live], [own_b, other_b, start, first_rate], size)

    received = exchange(other_q)
    stacked = jnp.concatenate(
        [own_q.reshape(comps * size // 2, size), received.reshape(comps * size // 2, size)], axis=0
    )
    place = jnp.zeros((size // 2,), jnp.int32).at[flat_order].set(
        jnp.arange(size // 2, dtype=jnp.int32)
    )
    wave_rows = wave_order.reshape(devices, 1, slots)
    row = jnp.take(place, wave_rows // 2)
    row = row + jnp.where(wave_rows % 2 == parity, 0, comps * size // 2)
    row = row + (size // 2) * jnp.arange(comps, dtype=jnp.int32)[None, :, None]
    leaving = jnp.take(stacked, row.reshape(-1), axis=0).reshape(devices, comps * slots, size)
    advanced = to_levels(leaving)

    lev_count = modes.shape[0] // levels
    rows_each = comps * slots // lev_count
    pieces = advanced.reshape(levels, lev_count, rows_each, size)
    gathered = lax.all_to_all(pieces, "lev", split_axis=1, concat_axis=0, tiled=True)
    gathered = gathered.reshape(levels * lev_count, rows_each, size)
    projected = jnp.einsum("lk,lrj->krj", modes, gathered, precision=HIGH_ACCURACY)
    waves = lax.dynamic_slice_in_dim(wave_order, wave_pos * slots, slots)
    block_waves = jnp.take(
        waves, (lev_pos * rows_each + jnp.arange(rows_each, dtype=jnp.int32)) % slots
    )
    degree = (block_waves[:, None] + every[None, :]).astype(jnp.float32)
    kappa = degree * (degree + 1.0) / (size * (size + 1.0))
    projected = projected / (kappa[None] + mode_rates[:, None, None])
    restored = jnp.einsum("lk,krj->lrj", modes, projected, precision=HIGH_ACCURACY)
    restored = restored * (degree < size - 0.5).astype(jnp.float32)
    stream = lax.all_to_all(
        restored.reshape(lev_count, levels, rows_each, size), "lev", split_axis=0, concat_axis=0, tiled=True
    )
    stream = jnp.moveaxis(stream.reshape(lev_count, levels, rows_each, size), 0, 1)
    stream = stream.reshape(levels, comps, slots, size)
    return (
        jnp.swapaxes(advanced.reshape(levels, comps, slots, size), 0, 1),
        jnp.swapaxes(stream, 0, 1),
    )


def on_any(vorticity, wind_lam, wind_mu, modes, mode_rates, wave_order, lat_order):
    comps, levels, slots, size = vorticity.shape
    devices = wave_order.shape[0] // slots
    lats, longitudes = lat_order.shape[0], wind_lam.shape[2]
    rows = comps * slots
    whole = (
        levels == devices
        and devices % 2 == 0
        and size == wave_order.shape[0]
        and size % (4 * GROUP) == 0
        and lats % 2 == 0
        and longitudes % 2 == 0
        and rows % (modes.shape[0] // levels) == 0
    )
    take = by_level if whole else on_device
    return take(vorticity, wind_lam, wind_mu, modes, mode_rates, wave_order, lat_order)


def solution(mesh):
    placed = (
        P(None, "lev", "wave", None),
        P("lev", "wave", None),
        P("lev", "wave", None),
        P(),
        P(),
        P(),
        P(),
    )
    return jax.shard_map(
        on_any,
        mesh=mesh,
        in_specs=placed,
        out_specs=(P(None, "lev", "wave", None), P(None, "lev", "wave", None)),
        check_vma=False,
    )
```

```python
import functools
import math

import jax
import jax.numpy as jnp
from jax import lax
from jax.experimental import pallas as pl
from jax.experimental.pallas import tpu as pltpu
from jax.sharding import PartitionSpec as P
import numpy as np

M = 640
LAT = 640
GRID_LONGITUDES = 1280


HIGH_ACCURACY = lax.Precision.HIGH
TIME_STEP = 0.4


def latitudes(lat_order):
    angles = math.pi * (lat_order.astype(jnp.float32) + 0.75) / (LAT + 0.5)
    sines = jnp.sin(angles)
    return (jnp.cos(angles), sines, math.pi / (LAT + 0.5) * sines)


GROUP = 8
PARTS = 2
LANES = 128
VMEM = 60 * 1024 * 1024


def table_kernel(ahead_ref, behind_ref, start_ref, cos_ref, out_ref):
    lats = out_ref.shape[2]
    spans = [(k, min(LANES, lats - k)) for k in range(0, lats, LANES)]
    mus = [jnp.broadcast_to(cos_ref[0:1, k : k + n], (GROUP, n)) for k, n in spans]

    def block(index, carry):
        first = pl.multiple_of(index * 8, 8)
        ahead = [ahead_ref[first + t] for t in range(8)]
        behind = [behind_ref[first + t] for t in range(8)]
        following_carry = []
        for (k, n), mu, (previous, current, log_scale) in zip(spans, mus, carry):
            scale = jnp.exp(log_scale)
            rows = []
            for t in range(8):
                rows.append(current * scale)
                following = ahead[t][:, :n] * (mu * current - behind[t][:, :n] * previous)
                previous, current = current, following
            magnitude = jnp.abs(previous) + jnp.abs(current)
            following_carry.append(
                (previous / magnitude, current / magnitude, log_scale + jnp.log(magnitude))
            )
            out_ref[:, pl.ds(first, 8), k : k + n] = jnp.swapaxes(jnp.stack(rows), 0, 1)
        return tuple(following_carry)

    initial = tuple(
        (
            jnp.zeros((GROUP, n), jnp.float32),
            jnp.ones((GROUP, n), jnp.float32),
            start_ref[:, k : k + n],
        )
        for k, n in spans
    )
    lax.fori_loop(0, out_ref.shape[1] // 8, block, initial)


def legendre(waves, cosines, sines, degrees):
    wavenum = waves.astype(jnp.float32)[:, None]
    counter = jnp.arange(1, M, dtype=jnp.int32).astype(jnp.float32)
    halves = 0.5 * jnp.log((2.0 * counter + 1.0) / (2.0 * counter))
    start_log = jnp.sum(jnp.where(counter[None, :] <= wavenum, halves[None, :], 0.0), axis=1)
    log_start = -0.5 * math.log(2.0) + start_log[:, None] + wavenum * jnp.log(sines)[None, :]
    degree = wavenum.T + jnp.arange(degrees, dtype=jnp.int32).astype(jnp.float32)[:, None] + 1.0
    square = wavenum.T * wavenum.T
    ahead = jnp.sqrt((4.0 * degree * degree - 1.0) / (degree * degree - square))
    lower = degree - 1.0
    behind = jnp.sqrt((lower * lower - square) / (4.0 * lower * lower - 1.0))
    slots, lats = waves.shape[0], cosines.shape[0]
    wide = (degrees, slots, LANES)
    coefficient = pl.BlockSpec((degrees, GROUP, LANES), lambda g: (0, g, 0))
    return pl.pallas_call(
        table_kernel,
        grid=(slots // GROUP,),
        in_specs=[
            coefficient,
            coefficient,
            pl.BlockSpec((GROUP, lats), lambda g: (g, 0)),
            pl.BlockSpec((1, lats), lambda g: (0, 0)),
        ],
        out_specs=pl.BlockSpec((GROUP, degrees, lats), lambda g: (g, 0, 0)),
        out_shape=jax.ShapeDtypeStruct((slots, degrees, lats), jnp.float32),
        compiler_params=pltpu.CompilerParams(vmem_limit_bytes=VMEM),
        name="table",
    )(
        jnp.broadcast_to(ahead[:, :, None], wide),
        jnp.broadcast_to(behind[:, :, None], wide),
        log_start,
        cosines[None, :],
    )


def halves_of(value):
    high = value.astype(jnp.bfloat16)
    return high, (value - high.astype(jnp.float32)).astype(jnp.bfloat16)


def three_products(fields, table, contract):
    rows = fields.shape[0]
    field_high, field_low = halves_of(fields)
    table_high, table_low = halves_of(table)
    dims = (((1,), (contract,)), ((), ()))
    both = lax.dot_general(
        jnp.concatenate([field_high, field_low], axis=0),
        table_high,
        dims,
        preferred_element_type=jnp.float32,
    )
    small = lax.dot_general(field_high, table_low, dims, preferred_element_type=jnp.float32)
    return both[:rows] + (both[rows:] + small)


def transform_kernel(waves_ref, fields_ref, table_ref, after_ref, out_ref, turned, result, *, forward):
    degrees = table_ref.shape[1]
    turned[...] = jnp.swapaxes(fields_ref[...], 0, 1)
    group = pl.program_id(0)

    def one_slot(i, carry):
        alive = degrees - waves_ref[group * GROUP + i]
        for first in range(0, degrees, 256):
            last = min(first + 256, degrees)

            @pl.when(alive > first)
            def _():
                table = table_ref[i, first:last, :]
                if forward:
                    result[i, :, first:last] = three_products(turned[i], table, 1)
                elif first == 0:
                    result[i] = three_products(turned[i, :, first:last], table, 0)
                else:
                    result[i] += three_products(turned[i, :, first:last], table, 0)

            if forward:

                @pl.when(alive <= first)
                def _():
                    result[i, :, first:last] = jnp.zeros(
                        (result.shape[1], last - first), jnp.float32
                    )

        return carry

    lax.fori_loop(0, GROUP, one_slot, 0)
    out_ref[...] = jnp.swapaxes(result[...], 0, 1)


def transform(waves, fields, table, after, forward):
    rows, slots, width = fields.shape
    degrees, lats = table.shape[1:]
    out_width = degrees if forward else lats
    return pl.pallas_call(
        functools.partial(transform_kernel, forward=forward),
        grid_spec=pltpu.PrefetchScalarGridSpec(
            num_scalar_prefetch=1,
            grid=(slots // GROUP,),
            in_specs=[
                pl.BlockSpec((rows, GROUP, width), lambda g, w: (0, g, 0)),
                pl.BlockSpec((GROUP, degrees, lats), lambda g, w: (g, 0, 0)),
                pl.BlockSpec(memory_space=pl.ANY),
            ],
            out_specs=pl.BlockSpec((rows, GROUP, out_width), lambda g, w: (0, g, 0)),
            scratch_shapes=[
                pltpu.VMEM((GROUP, rows, width), jnp.float32),
                pltpu.VMEM((GROUP, rows, out_width), jnp.float32),
            ],
        ),
        out_shape=jax.ShapeDtypeStruct((rows, slots, out_width), jnp.float32),
        compiler_params=pltpu.CompilerParams(vmem_limit_bytes=VMEM),
        name="analysis" if forward else "synthesis",
    )(waves, fields, table, after)


def padded(array, axis, size):
    widths = [(0, 0)] * array.ndim
    widths[axis] = (0, size - array.shape[axis])
    return jnp.pad(array, widths) if size > array.shape[axis] else array


def coupling(waves):
    wavenum = waves.astype(jnp.float32)[:, None]
    degree = wavenum + jnp.arange(M, dtype=jnp.int32).astype(jnp.float32)[None, :]
    live_mask = (degree < M - 0.5).astype(jnp.float32)
    square = wavenum * wavenum
    eps_here = jnp.sqrt((degree * degree - square) / (4.0 * degree * degree - 1.0))
    degree_next = degree + 1.0
    eps_ahead = jnp.sqrt(
        (degree_next * degree_next - square) / (4.0 * degree_next * degree_next - 1.0)
    )
    kappa = degree * (degree + 1.0) / (M * (M + 1.0))
    return (
        -(degree - 1.0) * eps_here * live_mask,
        (degree + 2.0) * eps_ahead * live_mask,
        live_mask,
        kappa,
    )


def fourier(waves):
    phase = waves[:, None] * jnp.arange(GRID_LONGITUDES, dtype=jnp.int32)[None, :] % GRID_LONGITUDES
    angles = 2.0 * math.pi / GRID_LONGITUDES * phase.astype(jnp.float32)
    return jnp.concatenate([jnp.cos(angles), jnp.sin(angles)], axis=0)


def lowered(spectra):
    return jnp.concatenate([jnp.zeros_like(spectra[..., :1]), spectra[..., :-1]], axis=-1)


def raised(spectra):
    return jnp.concatenate([spectra[..., 1:], jnp.zeros_like(spectra[..., :1])], axis=-1)


def on_device(vorticity, wind_lam, wind_mu, modes, mode_rates, wave_order, lat_order):
    slots = vorticity.shape[2]
    wave_pos = lax.axis_index("wave")
    lev_pos = lax.axis_index("lev")
    waves = lax.dynamic_slice_in_dim(wave_order, wave_pos * slots, slots)
    cosines, sines, weights = latitudes(lat_order)
    full = -(-slots // GROUP) * GROUP
    full_waves = padded(waves, 0, full)
    legendre_table = legendre(full_waves, cosines, sines, M)
    lower, upper, live_mask, kappa = coupling(waves)
    trigonometric_table = fourier(wave_order)
    double = jnp.where(wave_order == 0, 1.0, 2.0).astype(jnp.float32)
    scaled = double * wave_order.astype(jnp.float32)

    def synthesis(spectra, after):
        meridional = lower * lowered(spectra) + upper * raised(spectra)
        both = jnp.stack([spectra, meridional])
        rows = both.shape[0] * both.shape[1] * both.shape[2]
        flat = padded(both.reshape(rows, slots, M), 1, full)
        at_lat = transform(full_waves, flat, legendre_table, after, False)[:, :slots]
        return at_lat.reshape(both.shape[:4] + (LAT,))

    def to_latitudes(at_lat):
        return lax.all_to_all(at_lat, "wave", split_axis=4, concat_axis=3, tiled=True)

    def products(at_lat, part_lam, part_mu):
        zonal = jnp.concatenate(
            [-(scaled[:, None] * at_lat[0, 1]), -(scaled[:, None] * at_lat[0, 0])], axis=1
        )
        merid = jnp.concatenate(
            [double[:, None] * at_lat[1, 0], -(double[:, None] * at_lat[1, 1])], axis=1
        )
        grid = jnp.einsum(
            "flsr,sk->flrk", jnp.stack([zonal, merid]), trigonometric_table, precision=HIGH_ACCURACY
        )
        source_term = -(part_lam * grid[0] + part_mu * grid[1])
        spectral_latitude_fields = (
            jnp.einsum("nqy,zy->nzq", source_term, trigonometric_table, precision=HIGH_ACCURACY)
            / GRID_LONGITUDES
        )
        return jnp.stack([spectral_latitude_fields[:, :M], -spectral_latitude_fields[:, M:]])

    def to_waves(returned):
        return lax.all_to_all(returned, "wave", split_axis=2, concat_axis=3, tiled=True)

    def analysis(returned, after):
        returned = returned * weights
        flat = padded(returned.reshape(-1, slots, LAT), 1, full)
        result = transform(full_waves, flat, legendre_table, after, True)[:, :slots]
        return result.reshape(returned.shape[:3] + (M,)) * live_mask

    def token(array):
        corner = array[(0,) * (array.ndim - 2)]
        return lax.slice(corner, (0, 0), (min(8, corner.shape[0]), min(LANES, corner.shape[1])))

    def ordered(array, earlier):
        return array + 0.0 * token(earlier)[0, 0]

    levels = vorticity.shape[1]
    step = levels // PARTS if levels % PARTS == 0 else levels
    parts = [slice(first, first + step) for first in range(0, levels, step)]
    lev_count = modes.shape[0] // levels
    grouped = modes.reshape(lev_count, levels, modes.shape[1])
    rows_of = [grouped[:, part].reshape(lev_count * step, -1) for part in parts]
    winds = [(wind_lam[part], wind_mu[part]) for part in parts]
    starts = [vorticity[:, part] * live_mask for part in parts]
    count = len(parts)
    last = cosines[None, :]

    at_lats = []
    for start in starts:
        at_lats.append(synthesis(start, last))
        last = token(at_lats[-1])
    landed = [token(cosines[None, None, :])]

    def in_turn(exchange, array):
        moved = exchange(ordered(array, landed[0]))
        landed[0] = token(moved)
        return moved

    at_lats = [in_turn(to_latitudes, at_lat) for at_lat in at_lats]
    rates = []
    for stage in range(2):
        returned = []
        for at_lat, wind in zip(at_lats, winds):
            returned.append(products(ordered(at_lat, last), *wind))
            last = token(returned[-1])
        returned = [in_turn(to_waves, piece) for piece in returned]
        at_lats = []
        for index in range(count):
            rate = analysis(returned[index], last)
            last = token(rate)
            rates.append(rate)
            if stage == 0:
                middle = starts[index] + TIME_STEP / M * rate
                at_lats.append(synthesis(middle, last))
                last = token(at_lats[-1])
        at_lats = [in_turn(to_latitudes, at_lat) for at_lat in at_lats]
    advanced_parts = [
        starts[index] + 0.5 * TIME_STEP / M * (rates[index] + rates[count + index])
        for index in range(count)
    ]
    def to_blocks(array):
        return lax.all_to_all(array, "lev", split_axis=3, concat_axis=1, tiled=True)

    projected = 0.0
    for advanced, rows in zip(advanced_parts, rows_of):
        gathered = in_turn(to_blocks, advanced)
        projected = projected + jnp.einsum(
            "lk,clsj->cksj", rows, gathered, precision=HIGH_ACCURACY
        )
    block_width = projected.shape[3]
    diffusion_block = lax.dynamic_slice_in_dim(kappa, lev_pos * block_width, block_width, 1)
    projected = projected / (diffusion_block[None, None] + mode_rates[None, :, None, None])
    streams = []
    for rows in rows_of:
        restored = jnp.einsum("lk,cksj->clsj", rows, projected, precision=HIGH_ACCURACY)
        streams.append(lax.all_to_all(restored, "lev", split_axis=1, concat_axis=3, tiled=True))
    advanced = jnp.concatenate(advanced_parts, axis=1)
    stream = jnp.concatenate(streams, axis=1) * live_mask
    return (advanced, stream)


def order_list(size):
    blocks = size // (2 * GROUP)
    first = np.arange(blocks // 2)[:, None, None]
    block = np.concatenate([first, blocks - 1 - first], axis=1)
    return (block * GROUP + np.arange(GROUP)[None, None, :]).astype(np.int32)


def packed_width(size):
    width = size + 2 * GROUP
    return width, -(-width // LANES) * LANES


def packed_coupling(parity, size):
    width, lanes = packed_width(size)
    orders = 2 * jnp.asarray(order_list(size)) + parity
    lane = lax.broadcasted_iota(jnp.int32, (orders.shape[0], GROUP, lanes), 2)
    split = size - 2 * GROUP * lax.broadcasted_iota(jnp.int32, lane.shape, 0)
    wave = jnp.where(lane < split, orders[:, 0, :, None], orders[:, 1, :, None])
    degree = wave + jnp.where(lane < split, lane, lane - split)
    live = (degree < size) & (lane < width)
    ahead_live = (degree + 1 < size) & (lane < width)
    wave, degree = wave.astype(jnp.float32), degree.astype(jnp.float32)
    square = wave * wave
    following = degree + 1.0
    here = jnp.sqrt((degree * degree - square) / (4.0 * degree * degree - 1.0))
    beyond = jnp.sqrt((following * following - square) / (4.0 * following * following - 1.0))
    lower = jnp.where(live, -(degree - 1.0) * here, 0.0)
    upper = jnp.where(ahead_live, (degree + 2.0) * beyond, 0.0)
    return lower, upper, live.astype(jnp.float32)


def recurrence_factors(parity, size):
    width, _ = packed_width(size)
    orders = 2 * jnp.asarray(order_list(size)) + parity
    shape = (orders.shape[0], width // 16, GROUP, 32)
    lane = lax.broadcasted_iota(jnp.int32, shape, 3)
    position = 16 * lax.broadcasted_iota(jnp.int32, shape, 1) + lane % 16
    split = size - 2 * GROUP * lax.broadcasted_iota(jnp.int32, shape, 0)
    wave = jnp.where(position < split, orders[:, None, 0, :, None], orders[:, None, 1, :, None])
    degree = wave + jnp.where(position < split, position, position - split)
    wave, degree = wave.astype(jnp.float32), degree.astype(jnp.float32)
    square, following = wave * wave, degree + 1.0
    ahead = (4.0 * following * following - 1.0) / (following * following - square)
    behind = (degree * degree - square) / (4.0 * degree * degree - 1.0)
    return jnp.sqrt(jnp.where(lane < 16, ahead, behind))


def half_table_kernel(coefficient_ref, start_ref, cos_ref, *refs, size, first_pair):
    high_ref, low_ref = refs[-2:]
    lats = cos_ref.shape[1]
    pair = pl.program_id(0) + first_pair
    spans = [(k, min(LANES, lats - k)) for k in range(0, lats, LANES)]
    mus = [jnp.broadcast_to(cos_ref[0:1, k : k + n], (GROUP, n)) for k, n in spans]
    blocks = coefficient_ref.shape[1]
    restart = size // 16 - pair

    def fresh(which, k, n):
        return (
            jnp.zeros((GROUP, n), jnp.float32),
            jnp.ones((GROUP, n), jnp.float32),
            start_ref[0, which, :, k : k + n],
        )

    def block(index, carry):
        first = pl.multiple_of(index * 16, 16)
        again = index == restart
        coefficients = coefficient_ref[0, index]
        ahead = [jnp.broadcast_to(coefficients[:, t : t + 1], (GROUP, LANES)) for t in range(16)]
        behind = [
            jnp.broadcast_to(coefficients[:, 16 + t : 17 + t], (GROUP, LANES)) for t in range(16)
        ]
        following_carry = []
        for (k, n), mu, old in zip(spans, mus, carry):
            previous, current, log_scale = [
                jnp.where(again, new, kept) for new, kept in zip(fresh(1, k, n), old)
            ]
            rows = []
            for t in range(16):
                if t % 8 == 0:
                    scale = jnp.exp(log_scale)
                rows.append(current * scale)
                following = ahead[t][:, :n] * (mu * current - behind[t][:, :n] * previous)
                previous, current = current, following
                if t % 8 == 7:
                    magnitude = jnp.abs(previous) + jnp.abs(current)
                    inverse = 1.0 / magnitude
                    previous, current = previous * inverse, current * inverse
                    log_scale = log_scale + jnp.log(magnitude)
            following_carry.append((previous, current, log_scale))
            values = jnp.concatenate(
                [
                    jnp.swapaxes(jnp.stack(rows[:8]), 0, 1),
                    jnp.swapaxes(jnp.stack(rows[8:]), 0, 1),
                ],
                axis=1,
            )
            high = values.astype(jnp.bfloat16)
            high_ref[0, :, pl.ds(first, 16), k : k + n] = high
            low_ref[0, :, pl.ds(first, 16), k : k + n] = (
                values - high.astype(jnp.float32)
            ).astype(jnp.bfloat16)
        return tuple(following_carry)

    lax.fori_loop(0, blocks, block, tuple(fresh(0, k, n) for k, n in spans))


def table_starts(parity, sines, size):
    orders = 2 * jnp.asarray(order_list(size)) + parity
    wavenum = orders.reshape(-1).astype(jnp.float32)[:, None]
    counter = jnp.arange(1, size, dtype=jnp.int32).astype(jnp.float32)
    halves = 0.5 * jnp.log((2.0 * counter + 1.0) / (2.0 * counter))
    start_log = jnp.sum(jnp.where(counter[None, :] <= wavenum, halves[None, :], 0.0), axis=1)
    log_start = -0.5 * math.log(2.0) + start_log[:, None] + wavenum * jnp.log(sines)[None, :]
    return log_start.reshape(orders.shape + (sines.shape[0],))


def half_table(factors, starts, cosines, size, first_pair, count, table=()):
    width, _ = packed_width(size)
    pairs, blocks = factors.shape[:2]
    lats = cosines.shape[0]
    shape = jax.ShapeDtypeStruct((pairs, GROUP, width, lats), jnp.bfloat16)
    table_spec = pl.BlockSpec((1, GROUP, width, lats), lambda g: (g + first_pair, 0, 0, 0))
    return pl.pallas_call(
        functools.partial(half_table_kernel, size=size, first_pair=first_pair),
        grid=(count,),
        in_specs=[
            pl.BlockSpec((1, blocks, GROUP, 32), lambda g: (g + first_pair, 0, 0, 0)),
            pl.BlockSpec((1, 2, GROUP, lats), lambda g: (g + first_pair, 0, 0, 0)),
            pl.BlockSpec((1, lats), lambda g: (0, 0)),
        ]
        + [pl.BlockSpec(memory_space=pl.ANY)] * len(table),
        out_specs=[table_spec, table_spec],
        out_shape=[shape, shape],
        input_output_aliases={3: 0, 4: 1} if table else {},
        compiler_params=pltpu.CompilerParams(vmem_limit_bytes=VMEM),
        cost_estimate=pl.CostEstimate(
            flops=count * GROUP * width * lats * 2000,
            bytes_accessed=count * GROUP * width * lats * 4,
            transcendentals=0,
        ),
        name="half_table",
    )(factors, starts, cosines[None, :], *table)


def split_halves(value):
    high = value.astype(jnp.bfloat16)
    return high, (value - high.astype(jnp.float32)).astype(jnp.bfloat16)


def visit_kernel(*refs, size, stage):
    refs = list(refs)
    high_ref, low_ref = refs.pop(0), refs.pop(0)
    pair = pl.program_id(0)
    width, lanes = packed_width(size)
    split = size - 2 * GROUP * pair
    lats = high_ref.shape[3]
    position = lax.broadcasted_iota(jnp.int32, (1, lanes), 1)
    in_first, even = position < split, position % 2 == 0
    picks = [in_first & even, in_first & ~even, ~in_first & even, ~in_first & ~even]
    step = TIME_STEP / size

    def multiply(fields, table_slot, chunks, contract):
        rows = fields.shape[0]
        field_high, field_low = split_halves(fields)
        both_fields = jnp.concatenate([field_high, field_low], axis=0)
        both = small = None
        dims = (((1,), (contract,)), ((), ()))
        for c0, c1 in chunks:
            table_high = high_ref[0, table_slot, c0:c1, :]
            table_low = low_ref[0, table_slot, c0:c1, :]
            if contract == 0:
                left, left_high = both_fields[:, c0:c1], field_high[:, c0:c1]
            else:
                left, left_high = both_fields, field_high
            part = lax.dot_general(left, table_high, dims, preferred_element_type=jnp.float32)
            part_small = lax.dot_general(
                left_high, table_low, dims, preferred_element_type=jnp.float32
            )
            if both is None:
                both, small = [part], [part_small]
            elif contract == 0:
                both, small = [both[0] + part], [small[0] + part_small]
            else:
                both, small = both + [part], small + [part_small]
        both = jnp.concatenate(both, axis=1) if len(both) > 1 else both[0]
        small = jnp.concatenate(small, axis=1) if len(small) > 1 else small[0]
        return both[:rows] + (both[rows:] + small)

    chunks = [(c0, min(c0 + 256, width)) for c0 in range(0, width, 256)]

    if stage != "last":
        lower_ref, upper_ref = refs.pop(0), refs.pop(0)
    live_ref = refs.pop(0)
    if stage == "first":
        own_q_ref, other_q_ref, start_ref, own_ref, other_ref, fields, firsts, seconds = refs
        padding = jnp.zeros((4, lanes - size), jnp.float32)
        fields[0] = jnp.swapaxes(own_q_ref[:, 0, 0], 0, 1)
        fields[1] = jnp.swapaxes(other_q_ref[:, 0, 0], 0, 1)
        fields[2] = jnp.swapaxes(own_q_ref[:, 0, 1], 0, 1)
        fields[3] = jnp.swapaxes(other_q_ref[:, 0, 1], 0, 1)
    elif stage == "middle":
        own_b_ref, other_b_ref, start_ref, rate_ref, own_ref, other_ref, fields, firsts, seconds = refs
    else:
        own_b_ref, other_b_ref, start_ref, rate_ref, own_ref, other_ref, fields, firsts, seconds = refs
    if stage != "first":
        fields[0] = jnp.swapaxes(own_b_ref[:, 0, 0], 0, 1)
        fields[1] = jnp.swapaxes(other_b_ref[:, 0, 0], 0, 1)
        fields[2] = jnp.swapaxes(own_b_ref[:, 0, 1], 0, 1)
        fields[3] = jnp.swapaxes(other_b_ref[:, 0, 1], 0, 1)

    def one_slot(slot, carry):
        live = live_ref[0, pl.ds(slot, 1), :]
        block_a = jnp.concatenate([fields[0, slot], fields[1, slot]], axis=0)
        block_b = jnp.concatenate([fields[2, slot], fields[3, slot]], axis=0)
        if stage == "first":
            block_a = jnp.concatenate([block_a, padding], axis=1)
            block_b = pltpu.roll(jnp.concatenate([block_b, padding], axis=1), split, 1)
            spectra = jnp.where(in_first, block_a, block_b) * live
            start_ref[0, slot] = spectra
        else:
            sides = []
            for block in (block_a, block_b):
                north, south = block[:, :lats], block[:, lats:]
                sides += [north + south, north - south]
            sums = multiply(jnp.concatenate(sides, axis=0), slot, chunks, 1)
            sums = jnp.concatenate(
                [sums, jnp.zeros((sums.shape[0], lanes - width), jnp.float32)], axis=1
            )
            rate = jnp.zeros((4, lanes), jnp.float32)
            for index, pick in enumerate(picks):
                rate = jnp.where(pick, sums[4 * index : 4 * index + 4], rate)
            rate = rate * live
            if stage == "middle":
                rate_ref[0, slot] = rate
                spectra = start_ref[0, slot] + step * rate
            else:
                spectra = start_ref[0, slot] + 0.5 * step * (rate_ref[0, slot] + rate)
        if stage == "last":
            firsts[slot, :4] = jnp.where(in_first, spectra, 0.0)[:, :size]
            turned = pltpu.roll(spectra, lanes - split, 1)
            seconds[slot, :4] = jnp.where(position < width - split, turned, 0.0)[:, :size]
        else:
            meridional = lower_ref[0, pl.ds(slot, 1), :] * pltpu.roll(
                spectra, 1, 1
            ) + upper_ref[0, pl.ds(slot, 1), :] * pltpu.roll(spectra, lanes - 1, 1)
            both = jnp.concatenate([spectra, meridional], axis=0)
            masked = jnp.concatenate([jnp.where(pick, both, 0.0) for pick in picks], axis=0)
            sums = multiply(masked, slot, chunks, 0)
            firsts[slot] = jnp.concatenate([sums[0:8] + sums[8:16], sums[0:8] - sums[8:16]], axis=1)
            seconds[slot] = jnp.concatenate(
                [sums[16:24] + sums[24:32], sums[16:24] - sums[24:32]], axis=1
            )
        return carry

    lax.fori_loop(0, GROUP, one_slot, 0, unroll=True)
    for which, result in ((0, firsts), (1, seconds)):
        turned = jnp.swapaxes(result[...], 0, 1)
        if stage == "last":
            own_ref[:, 0, which] = turned[0:2]
            other_ref[:, 0, which] = turned[2:4]
        else:
            own_ref[0:2, 0, which] = turned[0:2]
            own_ref[2:4, 0, which] = turned[4:6]
            other_ref[0:2, 0, which] = turned[2:4]
            other_ref[2:4, 0, which] = turned[6:8]


def visit(stage, table, tables, arrays, size):
    width, lanes = packed_width(size)
    pairs, lats = table[0].shape[0], table[0].shape[3]
    table_spec = pl.BlockSpec((1, GROUP, width, lats), lambda g: (g, 0, 0, 0))
    row_spec = pl.BlockSpec((1, GROUP, lanes), lambda g: (g, 0, 0))
    packed_spec = pl.BlockSpec((1, GROUP, 4, lanes), lambda g: (g, 0, 0, 0))
    packed = jax.ShapeDtypeStruct((pairs, GROUP, 4, lanes), jnp.float32)

    def slots_spec(rows, columns):
        return pl.BlockSpec((rows, 1, 2, GROUP, columns), lambda g: (0, g, 0, 0, 0))

    def slots_shape(rows, columns):
        return jax.ShapeDtypeStruct((rows, pairs, 2, GROUP, columns), jnp.float32)

    at_lat = [slots_spec(4, 2 * lats)] * 2
    at_lat_shape = [slots_shape(4, 2 * lats)] * 2
    if stage == "first":
        in_columns, out_columns, out_rows = size, 2 * lats, 8
        specs = [row_spec] * 3 + [slots_spec(2, size)] * 2
        out_specs, out_shape = [packed_spec] + at_lat, [packed] + at_lat_shape
    elif stage == "middle":
        in_columns, out_columns, out_rows = 2 * lats, 2 * lats, 8
        specs = [row_spec] * 3 + [slots_spec(2, 2 * lats)] * 2 + [packed_spec]
        out_specs, out_shape = [packed_spec] + at_lat, [packed] + at_lat_shape
    else:
        in_columns, out_columns, out_rows = 2 * lats, size, 4
        specs = [row_spec] + [slots_spec(2, 2 * lats)] * 2 + [packed_spec] * 2
        out_specs, out_shape = [slots_spec(2, size)] * 2, [slots_shape(2, size)] * 2
    return pl.pallas_call(
        functools.partial(visit_kernel, size=size, stage=stage),
        grid=(pairs,),
        in_specs=[table_spec] * 2 + specs,
        out_specs=out_specs,
        out_shape=out_shape,
        scratch_shapes=[
            pltpu.VMEM((4, GROUP, 2, in_columns), jnp.float32),
            pltpu.VMEM((GROUP, out_rows, out_columns), jnp.float32),
            pltpu.VMEM((GROUP, out_rows, out_columns), jnp.float32),
        ],
        compiler_params=pltpu.CompilerParams(vmem_limit_bytes=VMEM),
        cost_estimate=pl.CostEstimate(
            flops=pairs * GROUP * width * lats * 2000,
            bytes_accessed=pairs * GROUP * width * lats * 4,
            transcendentals=0,
        ),
        name="visit_" + stage,
    )(*table, *tables, *arrays)


def by_level(vorticity, wind_lam, wind_mu, modes, mode_rates, wave_order, lat_order):
    comps, levels, slots, size = vorticity.shape
    lat_slots, longitudes = wind_lam.shape[1:]
    lats = lat_order.shape[0]
    half_lats, half_lons = lats // 2, longitudes // 2
    devices = levels
    wave_pos = lax.axis_index("wave")
    lev_pos = lax.axis_index("lev")
    parity = wave_pos % 2
    swap = [(d, d ^ 1) for d in range(devices)]

    def exchange(array):
        return lax.ppermute(array, "wave", swap)

    def to_levels(array):
        return lax.all_to_all(array, "wave", split_axis=0, concat_axis=0, tiled=True)

    every = jnp.arange(size, dtype=jnp.int32)

    def places(values, order):
        spots = jnp.arange(order.shape[0], dtype=jnp.int32)[None, :]
        return jnp.sum(jnp.where(order[None, :] == values[:, None], spots, 0), axis=1)

    def take_rows(array, rows):
        return array.at[rows].get(mode="promise_in_bounds")

    order = order_list(size)
    pairs = order.shape[0]
    flat_order = jnp.asarray(order.reshape(-1))

    spread = to_levels(jnp.swapaxes(vorticity, 0, 1)).reshape(devices * comps * slots, size)

    def rows_of(which):
        slot = places(2 * flat_order + which, wave_order)
        row = (slot // slots) * (comps * slots) + slot % slots
        rows = take_rows(spread, jnp.concatenate([row, row + slots]))
        return rows.reshape(comps, pairs, 2, GROUP, size)

    north = jnp.arange(half_lats, dtype=jnp.int32)
    cosines, sines, weights = latitudes(north)
    lower, upper, live = packed_coupling(parity, size)
    factors = recurrence_factors(parity, size)
    starts = table_starts(parity, sines, size)
    table = half_table(factors, starts, cosines, size, 0, pairs // 2)
    winds = jnp.concatenate([wind_lam, wind_mu], axis=1)
    winds = winds + 0.0 * (spread[0, 0] + table[0][0, 0, 0, 0].astype(jnp.float32))
    winds = to_levels(winds).reshape(2 * lats, longitudes)
    table = half_table(
        factors, starts, cosines, size, pairs // 2, pairs - pairs // 2, tuple(table)
    )

    lat_slot = places(jnp.concatenate([north, lats - 1 - north]), lat_order)
    lat_rows = (lat_slot // lat_slots) * (2 * lat_slots) + lat_slot % lat_slots

    sign = 1.0 - 2.0 * parity.astype(jnp.float32)
    row_scale = jnp.concatenate([weights, weights])[:, None] / longitudes

    def trigonometric(which):
        waves = 2 * flat_order + which
        phase = waves[:, None] * jnp.arange(half_lons, dtype=jnp.int32)[None, :] % longitudes
        angles = 2.0 * math.pi / longitudes * phase.astype(jnp.float32)
        cos, sin = jnp.cos(angles), jnp.sin(angles)
        double = jnp.where(waves == 0, 1.0, 2.0).astype(jnp.float32)[:, None]
        scaled = double * waves.astype(jnp.float32)[:, None]
        zonal = jnp.concatenate([-scaled * sin, -scaled * cos], axis=0)
        merid = jnp.concatenate([double * cos, -double * sin], axis=0)
        back = jnp.concatenate([cos, -sin], axis=0)
        return zonal, merid, back

    trig_own, trig_other = trigonometric(parity), trigonometric(1 - parity)

    def tendency_rows(own, other, wind_l, wind_m):
        received = exchange(other)

        def grid(field, table_own, table_other):
            mine = own[2 * field : 2 * field + 2].reshape(size, lats)
            theirs = received[2 * field : 2 * field + 2].reshape(size, lats)
            here = jnp.einsum("sr,sk->rk", mine, table_own, precision=HIGH_ACCURACY)
            there = jnp.einsum("sr,sk->rk", theirs, table_other, precision=HIGH_ACCURACY)
            return here + there, sign * (here - there)

        lam_near, lam_far = grid(0, trig_own[0], trig_other[0])
        mu_near, mu_far = grid(1, trig_own[1], trig_other[1])
        near = -(wind_l[:, :half_lons] * lam_near + wind_m[:, :half_lons] * mu_near) * row_scale
        far = -(wind_l[:, half_lons:] * lam_far + wind_m[:, half_lons:] * mu_far) * row_scale
        far = sign * far

        def back(folded, table_back):
            rows = jnp.einsum("zk,rk->zr", table_back, folded, precision=HIGH_ACCURACY)
            return rows.reshape(comps, pairs, 2, GROUP, lats)

        other_rows = exchange(back(near - far, trig_other[2]))
        own_rows = back(near + far, trig_own[2])
        return own_rows, other_rows

    own_q, other_q = rows_of(parity), exchange(rows_of(1 - parity))
    start, own_a, other_a = visit("first", table, [lower, upper, live], [own_q, other_q], size)
    wind_l, wind_m = take_rows(winds, lat_rows), take_rows(winds, lat_rows + lat_slots)
    own_b, other_b = tendency_rows(own_a, other_a, wind_l, wind_m)
    first_rate, own_a, other_a = visit(
        "middle", table, [lower, upper, live], [own_b, other_b, start], size
    )
    own_b, other_b = tendency_rows(own_a, other_a, wind_l, wind_m)
    own_q, other_q = visit("last", table, [live], [own_b, other_b, start, first_rate], size)

    received = exchange(other_q)
    stacked = jnp.concatenate(
        [own_q.reshape(comps * size // 2, size), received.reshape(comps * size // 2, size)], axis=0
    )
    wave_rows = wave_order.reshape(devices, 1, slots)
    row = places(wave_order // 2, flat_order).reshape(devices, 1, slots)
    row = row + jnp.where(wave_rows % 2 == parity, 0, comps * size // 2)
    row = row + (size // 2) * jnp.arange(comps, dtype=jnp.int32)[None, :, None]
    leaving = take_rows(stacked, row.reshape(-1)).reshape(devices, comps * slots, size)
    advanced = to_levels(leaving)

    lev_count = modes.shape[0] // levels
    rows_each = comps * slots // lev_count
    pieces = advanced.reshape(levels, lev_count, rows_each, size)
    gathered = lax.all_to_all(pieces, "lev", split_axis=1, concat_axis=0, tiled=True)
    gathered = gathered.reshape(levels * lev_count, rows_each, size)
    projected = jnp.einsum("lk,lrj->krj", modes, gathered, precision=HIGH_ACCURACY)
    waves = lax.dynamic_slice_in_dim(wave_order, wave_pos * slots, slots)
    block_waves = jnp.take(
        waves, (lev_pos * rows_each + jnp.arange(rows_each, dtype=jnp.int32)) % slots
    )
    degree = (block_waves[:, None] + every[None, :]).astype(jnp.float32)
    kappa = degree * (degree + 1.0) / (size * (size + 1.0))
    projected = projected / (kappa[None] + mode_rates[:, None, None])
    restored = jnp.einsum("lk,krj->lrj", modes, projected, precision=HIGH_ACCURACY)
    restored = restored * (degree < size - 0.5).astype(jnp.float32)
    stream = lax.all_to_all(
        restored.reshape(lev_count, levels, rows_each, size), "lev", split_axis=0, concat_axis=0, tiled=True
    )
    stream = jnp.moveaxis(stream.reshape(lev_count, levels, rows_each, size), 0, 1)
    stream = stream.reshape(levels, comps, slots, size)
    return (
        jnp.swapaxes(advanced.reshape(levels, comps, slots, size), 0, 1),
        jnp.swapaxes(stream, 0, 1),
    )


def on_any(vorticity, wind_lam, wind_mu, modes, mode_rates, wave_order, lat_order):
    comps, levels, slots, size = vorticity.shape
    devices = wave_order.shape[0] // slots
    lats, longitudes = lat_order.shape[0], wind_lam.shape[2]
    rows = comps * slots
    whole = (
        levels == devices
        and devices % 2 == 0
        and size == wave_order.shape[0]
        and size % (4 * GROUP) == 0
        and lats % 2 == 0
        and longitudes % 2 == 0
        and rows % (modes.shape[0] // levels) == 0
    )
    take = by_level if whole else on_device
    return take(vorticity, wind_lam, wind_mu, modes, mode_rates, wave_order, lat_order)


def solution(mesh):
    placed = (
        P(None, "lev", "wave", None),
        P("lev", "wave", None),
        P("lev", "wave", None),
        P(),
        P(),
        P(),
        P(),
    )
    return jax.shard_map(
        on_any,
        mesh=mesh,
        in_specs=placed,
        out_specs=(P(None, "lev", "wave", None), P(None, "lev", "wave", None)),
        check_vma=False,
    )
```
